32 devices in a mesh: grp: 2 (over y), col: 4 (over z), row: 2 (over x), limb: 2 (over core).
Axes of the slice: x: 2, y: 2, z: 4, core: 2. Of those that a mesh axis runs over, the one named last changes fastest.
Arguments:
- database: bfloat16 [8192, 8192], P(('grp', 'row'), 'col'), parts along dimension 0, may hold values from -128 to 127, as said below
- lwe_matrix: bfloat16 [8192, 2, 512], P('col', 'limb'), may hold values from -0.0008544922 to 0.0008544922
- secret_ct: float32 [2, 2, 2, 512, 4096], P(None, None, 'limb', 'col', 'row'), may hold values from -6 to 6
Outputs:
- encrypted_product: float32 [4, 2, 4096], P('grp', None, 'row'), parts along dimension 0
The draws below stay inside these ranges and needn't reach their ends.
There are 2 independent parts, one for each index of `grp`. The reference program is written for one: setup_inputs(seed, part) draws one part's arguments, and reference() takes and returns one part's arrays. A program takes and returns all parts, laid end to end along the dimension named above; an argument that names none is the same for every part. Nothing has to cross between parts.
Inputs may be any that keep to these rules, and one draw needn't show every extreme that they name: `database`: whole numbers.
All inputs are finite; a program needn't handle non-finite values.
Results may differ from the reference program's by a relative error of at most 0.0003.
Values sent between devices are 32-bit elements; how exact they have to be, the bound alone decides.
A program may use at most 64 MiB of HBM per device.

```python
import math
import jax
import jax.numpy as jnp
from jax import lax

DEGREE = 4096
HALF = 512
COLUMNS = 8192
N_ROW = 2


def draw_database(key, part):
    values = jax.random.randint(key, (DEGREE, COLUMNS), -128, 128)
    return values.astype(jnp.float32).astype(jnp.bfloat16)


def level_of(stream_key, extent, shards, smallest, largest):
    def one(axis_at, blocks):
        heights = jax.random.uniform(jax.random.fold_in(jax.random.fold_in(stream_key, 6), axis_at), (blocks,), jnp.float32, smallest / len(shards), largest / len(shards))
        return jnp.repeat(jnp.exp(heights), extent[axis_at] // blocks).reshape((-1,) + (1,) * (len(extent) - axis_at - 1))

    factor_of = one(*shards[0])
    for cut in shards[1:]:
        factor_of = factor_of * one(*cut)
    return factor_of


def noise(stream_key, extent, scale, reach, pieces=(), held_as=jnp.bfloat16):
    gain = level_of(stream_key, extent, pieces, -0.22, 0.18) if pieces else 1.0
    result = jax.random.normal(stream_key, extent, jnp.float32) * scale * gain
    return jnp.minimum(jnp.maximum(result, -reach), reach).astype(held_as)


def setup_inputs(seed: int = 0, part: int = 0) -> dict:
    seeds = jax.random.split(jax.random.key(seed), 4)
    part_splits = jax.random.split(jax.random.fold_in(seeds[3], part), 4)
    return {
        "database": draw_database(jax.random.fold_in(jax.random.fold_in(seeds[3], part), 71), part),
        "lwe_matrix": noise(seeds[1], (COLUMNS, 2, HALF), (COLUMNS * 5461) ** -0.5, 0.0008544922, ((0, 4), (1, 2))),
        "secret_ct": noise(seeds[2], (2, 2, 2, HALF, DEGREE), 1.0, 6.0, ((2, 2), (3, 4), (4, 2)), jnp.float32),
    }


def reference(database, lwe_matrix, secret_ct):
    hint_full = jnp.dot(database, lwe_matrix.reshape(COLUMNS, 2 * HALF), preferred_element_type=jnp.float32)
    row_index = jnp.arange(DEGREE).astype(hint_full.dtype)
    twist_factor = jnp.exp(-1j * jnp.pi * row_index / DEGREE)
    spectrum = jnp.fft.fft(hint_full * twist_factor[:, None], axis=0) / math.sqrt(DEGREE)
    spectrum = spectrum.reshape(DEGREE // N_ROW, N_ROW, 2 * HALF).transpose(1, 0, 2).reshape(DEGREE, 2 * HALF)
    real_part = jnp.real(spectrum).T
    imag_part = jnp.imag(spectrum).T
    cipher = secret_ct.reshape(2, 2, 2 * HALF, DEGREE)
    out_real = lax.optimization_barrier(jnp.sum(real_part * cipher[:, 0] - imag_part * cipher[:, 1], axis=1))
    out_imag = lax.optimization_barrier(jnp.sum(real_part * cipher[:, 1] + imag_part * cipher[:, 0], axis=1))
    return jnp.stack([out_real, out_imag], axis=1) / math.sqrt(2 * HALF)
```

```python
import math

import jax
import jax.numpy as jnp
import numpy as np
from jax import lax
from jax.sharding import PartitionSpec as P

CHUNKS = 4


def tables(row_count, row_dev, fast):
    slow = row_dev // fast
    degree = row_count * row_dev
    m = np.arange(row_dev)
    t = np.arange(fast)
    angle = -2.0 * np.pi * (m[:, None] * t[None, :] % row_dev) / row_dev
    first = np.exp(1j * angle).reshape(fast, slow, fast).transpose(1, 0, 2)
    a = np.arange(row_count)
    n = np.arange(degree)
    turn = -np.pi * (n[None, :] * (2 * a[:, None] + 1) % (2 * degree)) / degree
    turn = np.exp(1j * turn).reshape(row_count, row_count, fast, slow).transpose(0, 3, 1, 2)
    v = np.arange(slow)
    last = np.exp(-2j * np.pi * (v[:, None] * v[None, :] % slow) / slow)
    last = np.stack([np.stack([last.real, last.imag], 0), np.stack([-last.imag, last.real], 0)], 0)
    return first, turn, last.astype(np.float32)


def body(database, lwe_matrix, secret_ct):
    row_count = lax.axis_size("row")
    row_rank = lax.axis_index("row")
    col_count = lax.axis_size("col")
    row_dev = database.shape[0]
    half = lwe_matrix.shape[2]
    own = half // col_count
    part = own // CHUNKS
    fast = 128
    slow = row_dev // fast
    first, turn, last = tables(row_count, row_dev, fast)
    f_re = jnp.asarray(first.real, jnp.float32)[:, None]
    f_im = jnp.asarray(first.imag, jnp.float32)[:, None]
    g_re = lax.dynamic_index_in_dim(jnp.asarray(turn.real, jnp.float32), row_rank, 0, False)[..., None]
    g_im = lax.dynamic_index_in_dim(jnp.asarray(turn.imag, jnp.float32), row_rank, 0, False)[..., None]
    stage = jnp.stack([f_re * g_re - f_im * g_im, f_re * g_im + f_im * g_re], axis=3)
    stage = stage.reshape(slow, row_count, fast, 2, fast)
    panel = lwe_matrix[:, 0, :].reshape(-1, col_count, own)
    scale = 1.0 / (math.sqrt(row_dev * row_count) * math.sqrt(2 * half))
    prod_real = prod_imag = 0.0
    for k in range(CHUNKS):
        piece = panel[:, :, k * part : (k + 1) * part].reshape(-1, col_count * part)
        partial = lax.dot_general(
            piece, database, (((0,), (1,)), ((), ())), preferred_element_type=jnp.float32
        )
        mine = lax.psum_scatter(partial, "col", scatter_dimension=0, tiled=True)
        blocks = [mine]
        for step in range(1, row_count):
            perm = [(i, (i + step) % row_count) for i in range(row_count)]
            blocks.append(lax.ppermute(mine, "row", perm))
        total = 0.0
        for step, block in enumerate(blocks):
            source = (row_rank - step) % row_count
            table = lax.dynamic_index_in_dim(stage, source, 1, False)
            total = total + jnp.einsum(
                "juv,vuct->vjct",
                block.reshape(part, fast, slow),
                table,
                precision=lax.Precision.HIGH,
                preferred_element_type=jnp.float32,
            )
        spec = jnp.einsum("vjct,cdvs->djst", total, last, precision=lax.Precision.HIGH)
        spec = spec.reshape(2, part, row_dev)
        cipher = secret_ct[:, :, 0, k * part : (k + 1) * part]
        prod_real += jnp.sum(spec[0] * cipher[:, 0] - spec[1] * cipher[:, 1], axis=1)
        prod_imag += jnp.sum(spec[0] * cipher[:, 1] + spec[1] * cipher[:, 0], axis=1)
    return lax.psum(jnp.stack([prod_real, prod_imag], axis=1) * scale, ("col", "limb"))


def solution(mesh):
    placed = (P(("grp", "row"), "col"), P("col", "limb", None), P(None, None, "limb", "col", "row"))
    return jax.shard_map(
        body, mesh=mesh, in_specs=placed, out_specs=P("grp", None, "row"), check_vma=False
    )
```

```python
import functools
import math

import jax
import jax.numpy as jnp
import numpy as np
from jax import lax
from jax.experimental import pallas as pl
from jax.experimental.pallas import tpu as pltpu
from jax.sharding import PartitionSpec as P

CHUNKS = 4
MESH = pl.DeviceIdType.MESH


def hint_kernel(cols, rows, a_ref, d_hbm, out_ref, d_buf, part, from_left, from_right,
                d_sem, send_sem, recv_sem, row_send, row_recv):
    me = lax.axis_index("col")
    row = lax.axis_index("row")
    own, width = part.shape[2:]
    has_left, has_right = me > 0, me < cols - 1
    loads = [
        pltpu.make_async_copy(d_hbm.at[pl.ds(k * width, width)], d_buf.at[k], d_sem.at[k])
        for k in range(CHUNKS)
    ]
    for load in loads:
        load.start()
    barrier = pltpu.get_barrier_semaphore()
    for there, side in ((has_left, -1), (has_right, 1)):
        @pl.when(there)
        def _():
            pl.semaphore_signal(barrier, inc=1, device_id={"col": me + side}, device_id_type=MESH)
    for step in range(1, rows):
        pl.semaphore_signal(
            barrier, inc=1, device_id={"row": lax.rem(row + step, rows)}, device_id_type=MESH
        )
    inner = has_left & has_right

    @pl.when(inner)
    def _():
        pl.semaphore_wait(barrier, rows + 1)

    @pl.when(jnp.logical_not(inner))
    def _():
        pl.semaphore_wait(barrier, rows - 1 + min(cols - 1, 1))

    def hop(k, d, side):
        landing = from_left if side > 0 else from_right
        lane = 0 if side > 0 else 1
        return pltpu.make_async_remote_copy(
            src_ref=part.at[k, d],
            dst_ref=landing.at[k, d],
            send_sem=send_sem.at[k, d],
            recv_sem=recv_sem.at[lane, k, d],
            device_id={"col": me + side},
            device_id_type=MESH,
        )

    def across(k, step):
        here = out_ref.at[row, :, pl.ds(k * width, width)]
        return pltpu.make_async_remote_copy(
            src_ref=here,
            dst_ref=here,
            send_sem=row_send.at[k, step - 1],
            recv_sem=row_recv.at[k, step - 1],
            device_id={"row": lax.rem(row + step, rows)},
            device_id_type=MESH,
        )

    for k in range(CHUNKS):
        loads[k].wait()
        part[k] = lax.dot_general(
            a_ref[...], d_buf[k], (((1,), (1,)), ((), ())), preferred_element_type=jnp.float32
        ).reshape(cols, own, width)

        @pl.when(me == 0)
        def _():
            for d in range(cols - 1, 0, -1):
                hop(k, d, 1).start()

        @pl.when(me == cols - 1)
        def _():
            for d in range(cols - 1):
                hop(k, d, -1).start()

    for k in range(CHUNKS):
        for i in range(cols - 1):
            right, left = cols - 1 - i, i

            @pl.when(has_left & (me < right))
            def _():
                hop(k, right, 1).wait_recv()
                part[k, right] += from_left[k, right]
                hop(k, right, 1).start()

            @pl.when(has_right & (me > left))
            def _():
                hop(k, left, -1).wait_recv()
                part[k, left] += from_right[k, left]
                hop(k, left, -1).start()

        @pl.when(has_left)
        def _():
            hop(k, me, 1).wait_recv()
            part[k, me] += from_left[k, me]

        @pl.when(has_right)
        def _():
            hop(k, me, -1).wait_recv()
            part[k, me] += from_right[k, me]

        out_ref[row, :, k * width : (k + 1) * width] = part[k, me]
        for step in range(1, rows):
            across(k, step).start()

    for k in range(CHUNKS):
        for d in range(cols):
            @pl.when(me != d)
            def _():
                hop(k, d, 1).wait_send()
        for step in range(1, rows):
            across(k, step).wait()


def gather_hint(panel, database, cols, rows):
    row_dev, depth = database.shape
    own, width = panel.shape[0] // cols, row_dev // CHUNKS
    blocks = pltpu.VMEM((CHUNKS, cols, own, width), jnp.float32)
    return pl.pallas_call(
        functools.partial(hint_kernel, cols, rows),
        out_shape=jax.ShapeDtypeStruct((rows, own, row_dev), jnp.float32),
        in_specs=[pl.BlockSpec(memory_space=pltpu.VMEM), pl.BlockSpec(memory_space=pl.ANY)],
        out_specs=pl.BlockSpec(memory_space=pltpu.VMEM),
        scratch_shapes=[
            pltpu.VMEM((CHUNKS, width, depth), database.dtype),
            blocks,
            blocks,
            blocks,
            pltpu.SemaphoreType.DMA((CHUNKS,)),
            pltpu.SemaphoreType.DMA((CHUNKS, cols)),
            pltpu.SemaphoreType.DMA((2, CHUNKS, cols)),
            pltpu.SemaphoreType.DMA((CHUNKS, max(rows - 1, 1))),
            pltpu.SemaphoreType.DMA((CHUNKS, max(rows - 1, 1))),
        ],
        compiler_params=pltpu.CompilerParams(
            collective_id=0, has_side_effects=True, vmem_limit_bytes=48 << 20
        ),
    )(panel, database)


def sum_kernel(cols, limbs, x_ref, out_ref, landed, send_sem, recv_sem):
    col, limb = lax.axis_index("col"), lax.axis_index("limb")
    count = cols * limbs
    me = col * limbs + limb
    peers = [lax.rem(me + step, count) for step in range(1, count)]
    barrier = pltpu.get_barrier_semaphore()
    copies = []
    for step, peer in enumerate(peers):
        where = {"col": peer // limbs, "limb": lax.rem(peer, limbs)}
        pl.semaphore_signal(barrier, inc=1, device_id=where, device_id_type=MESH)
        copies.append(
            pltpu.make_async_remote_copy(
                src_ref=x_ref,
                dst_ref=landed.at[step],
                send_sem=send_sem.at[step],
                recv_sem=recv_sem.at[step],
                device_id=where,
                device_id_type=MESH,
            )
        )
    pl.semaphore_wait(barrier, count - 1)
    for copy in copies:
        copy.start()
    total = x_ref[...]
    for step, copy in enumerate(copies):
        copy.wait()
        total = total + landed[step]
    out_ref[...] = total


def sum_all(x, cols, limbs):
    peers = cols * limbs - 1
    return pl.pallas_call(
        functools.partial(sum_kernel, cols, limbs),
        out_shape=jax.ShapeDtypeStruct(x.shape, x.dtype),
        in_specs=[pl.BlockSpec(memory_space=pltpu.VMEM)],
        out_specs=pl.BlockSpec(memory_space=pltpu.VMEM),
        scratch_shapes=[
            pltpu.VMEM((peers,) + x.shape, x.dtype),
            pltpu.SemaphoreType.DMA((peers,)),
            pltpu.SemaphoreType.DMA((peers,)),
        ],
        compiler_params=pltpu.CompilerParams(collective_id=1, has_side_effects=True),
    )(x)


def tables(row_count, row_dev, fast):
    slow = row_dev // fast
    degree = row_count * row_dev
    m = np.arange(row_dev)
    t = np.arange(fast)
    angle = -2.0 * np.pi * (m[:, None] * t[None, :] % row_dev) / row_dev
    first = np.exp(1j * angle).reshape(fast, slow, fast).transpose(1, 0, 2)
    a = np.arange(row_count)
    n = np.arange(degree)
    turn = -np.pi * (n[None, :] * (2 * a[:, None] + 1) % (2 * degree)) / degree
    turn = np.exp(1j * turn).reshape(row_count, row_count, fast, slow).transpose(0, 3, 1, 2)
    v = np.arange(slow)
    last = np.exp(-2j * np.pi * (v[:, None] * v[None, :] % slow) / slow)
    last = np.stack([np.stack([last.real, last.imag], 0), np.stack([-last.imag, last.real], 0)], 0)
    return first, turn, last.astype(np.float32)


def body(database, lwe_matrix, secret_ct):
    row_count = lax.axis_size("row")
    row_rank = lax.axis_index("row")
    col_count = lax.axis_size("col")
    row_dev = database.shape[0]
    half = lwe_matrix.shape[2]
    own = half // col_count
    fast = 128
    slow = row_dev // fast
    first, turn, last = tables(row_count, row_dev, fast)
    f_re = jnp.asarray(first.real, jnp.float32)[:, None]
    f_im = jnp.asarray(first.imag, jnp.float32)[:, None]
    g_re = lax.dynamic_index_in_dim(jnp.asarray(turn.real, jnp.float32), row_rank, 0, False)[..., None]
    g_im = lax.dynamic_index_in_dim(jnp.asarray(turn.imag, jnp.float32), row_rank, 0, False)[..., None]
    stage = jnp.stack([f_re * g_re - f_im * g_im, f_re * g_im + f_im * g_re], axis=3)
    stage = stage.reshape(slow, row_count, fast, 2, fast)
    blocks = gather_hint(lwe_matrix[:, 0, :].T, database, col_count, row_count)
    total = 0.0
    for source in range(row_count):
        total = total + jnp.einsum(
            "juv,vuct->vjct",
            blocks[source].reshape(own, fast, slow),
            stage[:, source],
            precision=lax.Precision.HIGH,
            preferred_element_type=jnp.float32,
        )
    spec = jnp.einsum("vjct,cdvs->djst", total, last, precision=lax.Precision.HIGH)
    spec = spec.reshape(2, own, row_dev)
    scale = 1.0 / (math.sqrt(row_dev * row_count) * math.sqrt(2 * half))
    cipher = secret_ct[:, :, 0]
    prod_real = jnp.sum(spec[0] * cipher[:, 0] - spec[1] * cipher[:, 1], axis=1)
    prod_imag = jnp.sum(spec[0] * cipher[:, 1] + spec[1] * cipher[:, 0], axis=1)
    product = jnp.concatenate([prod_real, prod_imag], axis=0) * scale
    product = sum_all(
        product.reshape(8, -1), col_count, lax.axis_size("limb")
    ).reshape(2, 2, row_dev)
    return jnp.swapaxes(product, 0, 1)


def solution(mesh):
    placed = (P(("grp", "row"), "col"), P("col", "limb", None), P(None, None, "limb", "col", "row"))
    return jax.shard_map(
        body, mesh=mesh, in_specs=placed, out_specs=P("grp", None, "row"), check_vma=False
    )
```

```python
import functools
import math

import jax
import jax.numpy as jnp
import numpy as np
from jax import lax
from jax.experimental import pallas as pl
from jax.experimental.pallas import tpu as pltpu
from jax.sharding import PartitionSpec as P

CHUNKS = 4
MESH = pl.DeviceIdType.MESH


def hint_kernel(cols, rows, a_ref, d_hbm, out_ref, d_buf, part, from_left, from_right,
                d_sem, send_sem, recv_sem, row_send, row_recv):
    me = lax.axis_index("col")
    row = lax.axis_index("row")
    own, width = part.shape[2:]
    has_left, has_right = me > 0, me < cols - 1
    loads = [
        pltpu.make_async_copy(d_hbm.at[pl.ds(k * width, width)], d_buf.at[k], d_sem.at[k])
        for k in range(CHUNKS)
    ]
    for load in loads:
        load.start()
    barrier = pltpu.get_barrier_semaphore()
    for there, side in ((has_left, -1), (has_right, 1)):
        @pl.when(there)
        def _():
            pl.semaphore_signal(barrier, inc=1, device_id={"col": me + side}, device_id_type=MESH)
    for step in range(1, rows):
        pl.semaphore_signal(
            barrier, inc=1, device_id={"row": lax.rem(row + step, rows)}, device_id_type=MESH
        )
    inner = has_left & has_right

    @pl.when(inner)
    def _():
        pl.semaphore_wait(barrier, rows + 1)

    @pl.when(jnp.logical_not(inner))
    def _():
        pl.semaphore_wait(barrier, rows - 1 + min(cols - 1, 1))

    def hop(k, d, side):
        landing = from_left if side > 0 else from_right
        lane = 0 if side > 0 else 1
        return pltpu.make_async_remote_copy(
            src_ref=part.at[k, d],
            dst_ref=landing.at[k, d],
            send_sem=send_sem.at[k, d],
            recv_sem=recv_sem.at[lane, k, d],
            device_id={"col": me + side},
            device_id_type=MESH,
        )

    def across(k, step):
        here = out_ref.at[row, :, pl.ds(k * width, width)]
        return pltpu.make_async_remote_copy(
            src_ref=here,
            dst_ref=here,
            send_sem=row_send.at[k, step - 1],
            recv_sem=row_recv.at[k, step - 1],
            device_id={"row": lax.rem(row + step, rows)},
            device_id_type=MESH,
        )

    for k in range(CHUNKS):
        loads[k].wait()
        part[k] = lax.dot_general(
            a_ref[...], d_buf[k], (((1,), (1,)), ((), ())), preferred_element_type=jnp.float32
        ).reshape(cols, own, width)

        @pl.when(me == 0)
        def _():
            for d in range(cols - 1, 0, -1):
                hop(k, d, 1).start()

        @pl.when(me == cols - 1)
        def _():
            for d in range(cols - 1):
                hop(k, d, -1).start()

    for k in range(CHUNKS):
        for i in range(cols - 1):
            right, left = cols - 1 - i, i

            @pl.when(has_left & (me < right))
            def _():
                hop(k, right, 1).wait_recv()
                part[k, right] += from_left[k, right]
                hop(k, right, 1).start()

            @pl.when(has_right & (me > left))
            def _():
                hop(k, left, -1).wait_recv()
                part[k, left] += from_right[k, left]
                hop(k, left, -1).start()

        @pl.when(has_left)
        def _():
            hop(k, me, 1).wait_recv()
            part[k, me] += from_left[k, me]

        @pl.when(has_right)
        def _():
            hop(k, me, -1).wait_recv()
            part[k, me] += from_right[k, me]

        out_ref[row, :, k * width : (k + 1) * width] = part[k, me]
        for step in range(1, rows):
            across(k, step).start()

    for k in range(CHUNKS):
        for d in range(cols):
            @pl.when(me != d)
            def _():
                hop(k, d, 1).wait_send()
        for step in range(1, rows):
            across(k, step).wait()


def gather_hint(panel, database, cols, rows):
    row_dev, depth = database.shape
    own, width = panel.shape[0] // cols, row_dev // CHUNKS
    blocks = pltpu.VMEM((CHUNKS, cols, own, width), jnp.float32)
    return pl.pallas_call(
        functools.partial(hint_kernel, cols, rows),
        out_shape=jax.ShapeDtypeStruct((rows, own, row_dev), jnp.float32),
        in_specs=[pl.BlockSpec(memory_space=pltpu.VMEM), pl.BlockSpec(memory_space=pl.ANY)],
        out_specs=pl.BlockSpec(memory_space=pltpu.VMEM),
        scratch_shapes=[
            pltpu.VMEM((CHUNKS, width, depth), database.dtype),
            blocks,
            blocks,
            blocks,
            pltpu.SemaphoreType.DMA((CHUNKS,)),
            pltpu.SemaphoreType.DMA((CHUNKS, cols)),
            pltpu.SemaphoreType.DMA((2, CHUNKS, cols)),
            pltpu.SemaphoreType.DMA((CHUNKS, max(rows - 1, 1))),
            pltpu.SemaphoreType.DMA((CHUNKS, max(rows - 1, 1))),
        ],
        compiler_params=pltpu.CompilerParams(
            collective_id=0, has_side_effects=True, vmem_limit_bytes=48 << 20
        ),
    )(panel, database)


def sum_kernel(cols, limbs, x_ref, out_ref, landed, send_sem, recv_sem):
    col, limb = lax.axis_index("col"), lax.axis_index("limb")
    count = cols * limbs
    me = col * limbs + limb
    peers = [lax.rem(me + step, count) for step in range(1, count)]
    barrier = pltpu.get_barrier_semaphore()
    copies = []
    for step, peer in enumerate(peers):
        where = {"col": peer // limbs, "limb": lax.rem(peer, limbs)}
        pl.semaphore_signal(barrier, inc=1, device_id=where, device_id_type=MESH)
        copies.append(
            pltpu.make_async_remote_copy(
                src_ref=x_ref,
                dst_ref=landed.at[step],
                send_sem=send_sem.at[step],
                recv_sem=recv_sem.at[step],
                device_id=where,
                device_id_type=MESH,
            )
        )
    pl.semaphore_wait(barrier, count - 1)
    for copy in copies:
        copy.start()
    total = x_ref[...]
    for step, copy in enumerate(copies):
        copy.wait()
        total = total + landed[step]
    out_ref[...] = total


def sum_all(x, cols, limbs):
    peers = cols * limbs - 1
    return pl.pallas_call(
        functools.partial(sum_kernel, cols, limbs),
        out_shape=jax.ShapeDtypeStruct(x.shape, x.dtype),
        in_specs=[pl.BlockSpec(memory_space=pltpu.VMEM)],
        out_specs=pl.BlockSpec(memory_space=pltpu.VMEM),
        scratch_shapes=[
            pltpu.VMEM((peers,) + x.shape, x.dtype),
            pltpu.SemaphoreType.DMA((peers,)),
            pltpu.SemaphoreType.DMA((peers,)),
        ],
        compiler_params=pltpu.CompilerParams(collective_id=1, has_side_effects=True),
    )(x)


def tables(row_count, row_dev, fast):
    slow = row_dev // fast
    degree = row_count * row_dev
    m = np.arange(row_dev)
    t = np.arange(fast)
    angle = -2.0 * np.pi * (m[:, None] * t[None, :] % row_dev) / row_dev
    first = np.exp(1j * angle).reshape(fast, slow, fast).transpose(1, 0, 2)
    first = np.stack([first.real, first.imag], 2).astype(np.float32)
    a = np.arange(row_count)
    n = np.arange(degree)
    turn = -np.pi * (n[None, :] * (2 * a[:, None] + 1) % (2 * degree)) / degree
    turn = np.exp(1j * turn).reshape(row_count, row_count, row_dev)
    turn = np.stack([turn.real, turn.imag], 1).astype(np.float32)
    v = np.arange(slow)
    last = np.exp(-2j * np.pi * (v[:, None] * v[None, :] % slow) / slow)
    last = np.stack([last, 1j * last], 0)
    last = np.stack([last, 1j * last], 0)
    last = np.stack([last.real, last.imag], 2).astype(np.float32)
    return first, turn, last


def body(database, lwe_matrix, secret_ct):
    row_count = lax.axis_size("row")
    row_rank = lax.axis_index("row")
    col_count = lax.axis_size("col")
    row_dev = database.shape[0]
    half = lwe_matrix.shape[2]
    own = half // col_count
    fast = 128
    slow = row_dev // fast
    first, turn, last = tables(row_count, row_dev, fast)
    blocks = gather_hint(lwe_matrix[:, 0, :].T, database, col_count, row_count)
    turn = lax.dynamic_index_in_dim(jnp.asarray(turn), row_rank, 0, False)
    turned = jnp.sum(blocks[None] * turn[:, :, None, :], axis=1)
    total = jnp.einsum(
        "zjuv,vuct->vzjct",
        turned.reshape(2, own, fast, slow),
        first,
        precision=lax.Precision.HIGH,
        preferred_element_type=jnp.float32,
    )
    spec = jnp.einsum("vzjct,zcdvs->djst", total, last, precision=lax.Precision.HIGH)
    spec = spec.reshape(2, own, row_dev)
    scale = 1.0 / (math.sqrt(row_dev * row_count) * math.sqrt(2 * half))
    cipher = secret_ct[:, :, 0]
    prod_real = jnp.sum(spec[0] * cipher[:, 0] - spec[1] * cipher[:, 1], axis=1)
    prod_imag = jnp.sum(spec[0] * cipher[:, 1] + spec[1] * cipher[:, 0], axis=1)
    product = jnp.concatenate([prod_real, prod_imag], axis=0) * scale
    product = sum_all(
        product.reshape(8, -1), col_count, lax.axis_size("limb")
    ).reshape(2, 2, row_dev)
    return jnp.swapaxes(product, 0, 1)


def solution(mesh):
    placed = (P(("grp", "row"), "col"), P("col", "limb", None), P(None, None, "limb", "col", "row"))
    return jax.shard_map(
        body, mesh=mesh, in_specs=placed, out_specs=P("grp", None, "row"), check_vma=False
    )
```
